256 devices in a mesh: grp: 8 (over z), own: 32 (over y, x, core).
Axes of the slice: x: 4, y: 4, z: 8, core: 2. Of those that a mesh axis runs over, the one named last changes fastest.
Arguments:
- embeddings: bfloat16 [262144, 1024], P(('grp', 'own')), may hold values from -6 to 6
- assign_one: int32 [262144], P(('grp', 'own')), may hold values from 0 to 2047, as said below
- candidates: int32 [32, 262144], P(None, ('grp', 'own')), may hold values from 0 to 2047, as said below
- centroids: bfloat16 [2048, 1024], P('own'), may hold values from -3 to 3
- parents: int32 [2048, 1], replicated, may hold values from 0 to 255
Outputs:
- new_centroids: float32 [2048, 1024], P('own')
- top_centroids: float32 [256, 1024], replicated
- candidate_dist: float32 [32, 262144], P(None, ('grp', 'own'))
The draws below stay inside these ranges and needn't reach their ends.
Inputs may be any that keep to these rules, and one draw needn't show every extreme that they name: `assign_one`: in each device's rows (aligned blocks of 1024 rows), at most 128 name a centroid of any one owner (ids o * 64 to (o + 1) * 64 - 1); one owner, the same in every block, is named by exactly 128. Each embedding's own level-one centroid (assign_one) is among its candidates. `parents`: every level-two id is named by some level-one centroid.
All inputs are finite; a program needn't handle non-finite values.
Results may differ from the reference program's by a relative error of at most 0.0003.
Values may be sent and summed in bfloat16 or wider, within the bound.
A program may use at most 64 MiB of HBM per device.

```python
import math
import jax
import jax.numpy as jnp
from jax import lax

D = 1024
ROWS_DEV = 1024
K1_DEV = 64
K2 = 256
NCAND = 32
K1 = 2048
CAP = 128
ROWS = 262144
N_GRP = 8
N_OWN = 32


def assign_labels(key):
    block_count = N_GRP * N_OWN
    hot_key, offset_key, block_key = jax.random.split(jax.random.fold_in(key, 11), 3)
    hot_owner = jax.random.randint(hot_key, (), 0, N_OWN)
    offsets = jax.random.randint(offset_key, (N_OWN,), 0, K1_DEV)
    block_keys = jax.random.split(block_key, block_count)
    spread = max(1, 3 * K1_DEV // 4)

    def one_block(one_key):
        key_order, key_shuffle, key_first, key_second = jax.random.split(one_key, 4)
        slot_list = jnp.arange(N_OWN * CAP, dtype=jnp.int32)
        slot_owner = slot_list // CAP
        ranking = jax.random.permutation(key_order, N_OWN * CAP).astype(jnp.int32)
        priority = jnp.where(slot_owner == hot_owner, -1, 0) * (N_OWN * CAP) + ranking
        chosen = jnp.argsort(priority, stable=True)[:ROWS_DEV]
        row_owner = jax.random.permutation(key_shuffle, slot_owner[chosen])
        low_one = jax.random.randint(key_first, (ROWS_DEV,), 0, spread)
        low_two = jax.random.randint(key_second, (ROWS_DEV,), 0, spread)
        within = (jnp.minimum(low_one, low_two) + offsets[row_owner]) % K1_DEV
        return (row_owner * K1_DEV + within).astype(jnp.int32)
    return lax.map(one_block, block_keys).reshape(-1)


def draw_assign_one(key, part):
    return assign_labels(key)


def draw_embeddings(key, part):
    labels = assign_labels(key)
    block_count = N_GRP * N_OWN
    base_key, noise_key = jax.random.split(jax.random.fold_in(key, 23), 2)
    centres = 0.8 * jnp.clip(jax.random.normal(base_key, (K1, D), jnp.float32), -3.0, 3.0)

    def one_block(block_index):
        start = (block_index * ROWS_DEV).astype(jnp.int32)
        rows = lax.dynamic_slice_in_dim(labels, start, ROWS_DEV, 0)
        centre_rows = jnp.take(centres, rows, axis=0)
        block_key = jax.random.fold_in(noise_key, block_index)
        second_key = jax.random.fold_in(block_key, 1)
        noise = 0.6 * jnp.clip(jax.random.normal(second_key, (ROWS_DEV, D), jnp.float32), -3.0, 3.0)
        return centre_rows + noise
    return lax.map(one_block, jnp.arange(block_count, dtype=jnp.int32)).reshape(ROWS, D).astype(jnp.bfloat16)


def draw_candidates(key, part):
    labels = assign_labels(key)
    pick_key, place_key = jax.random.split(jax.random.fold_in(key, 37), 2)
    random_ids = jax.random.randint(pick_key, (NCAND, ROWS), 0, K1)
    place = jax.random.randint(place_key, (ROWS,), 0, NCAND)
    own_slot = jnp.arange(NCAND, dtype=jnp.int32)[:, None] == place[None, :]
    return jnp.where(own_slot, labels[None, :], random_ids).astype(jnp.int32)


def levels(key, shape, cuts, low, largest):
    def one(axis_at, shards_of):
        heights = jax.random.uniform(jax.random.fold_in(jax.random.fold_in(key, 6), axis_at), (shards_of,), jnp.float32, low / len(cuts), largest / len(cuts))
        return jnp.repeat(jnp.exp(heights), shape[axis_at] // shards_of).reshape((-1,) + (1,) * (len(shape) - axis_at - 1))

    gain = one(*cuts[0])
    for cut in cuts[1:]:
        gain = gain * one(*cut)
    return gain


def choose_distinct(key, rows, number_of, top, lift):
    sequence = jax.random.permutation(jax.random.fold_in(key, 1), number_of)
    boost = sequence
    for power in range(3):
        boost = boost * boost // number_of
    boost = boost * lift // number_of
    tickets = jax.random.randint(jax.random.fold_in(key, 2), (rows, number_of), 0, 4096) + boost
    fixed_rows = jax.random.permutation(jax.random.fold_in(key, 3), rows)[jnp.arange(number_of) % rows]
    tickets = jnp.where(jnp.arange(rows)[:, None] == fixed_rows[None, :], 1 << 14, tickets)
    merit = tickets * number_of + jnp.arange(number_of)
    return lax.top_k(merit.astype(jnp.int32), top)[1].astype(jnp.int32)


def centred(own_key, shape, width, bound, shards=(), kind=jnp.bfloat16):
    result = jax.random.normal(own_key, shape, jnp.float32) * width
    if len(shards) > 0:
        result = levels(own_key, shape, shards, -0.22, 0.18) * result
    return jnp.clip(result, min=-bound, max=bound).astype(kind)


def setup_inputs(seed: int = 0) -> dict:
    splits = jax.random.split(jax.random.key(seed), 6)
    return {
        "embeddings": draw_embeddings(jax.random.fold_in(splits[5], 71), 0),
        "assign_one": draw_assign_one(jax.random.fold_in(splits[5], 71), 0),
        "candidates": draw_candidates(jax.random.fold_in(splits[5], 71), 0),
        "centroids": centred(splits[3], (K1, D), 0.5, 3.0, ((0, 32),)),
        "parents": choose_distinct(splits[4], K1, K2, 1, 0),
    }


def reference(embeddings, assign_one, candidates, centroids, parents):
    row_total = embeddings.shape[0]
    block_rows = math.gcd(row_total, 8192)

    def absorb(carry, block_index):
        running, tallies = carry
        start = (block_index * block_rows).astype(jnp.int32)
        features = lax.dynamic_slice_in_dim(embeddings, start, block_rows, 0).astype(jnp.float32)
        labels = lax.dynamic_slice_in_dim(assign_one, start, block_rows, 0)
        running = running + jax.ops.segment_sum(features, labels, num_segments=K1)
        tallies = tallies + jax.ops.segment_sum(jnp.ones((block_rows,), jnp.float32), labels, num_segments=K1)
        return (running, tallies), None

    start_state = (jnp.zeros((K1, D), jnp.float32), jnp.zeros((K1,), jnp.float32))
    (cluster_sums, counts), _ = lax.scan(absorb, start_state, jnp.arange(row_total // block_rows, dtype=jnp.int32))
    previous = centroids.astype(jnp.float32)
    new_centroids = jnp.where(counts[:, None] > 0, cluster_sums / jnp.maximum(counts, 1.0)[:, None], previous)
    rounded = new_centroids.astype(jnp.bfloat16)
    rounded_norms = jnp.sum(jnp.square(rounded.astype(jnp.float32)), axis=1)
    parent_ids = parents[:, 0]
    parent_total = jax.ops.segment_sum(new_centroids, parent_ids, num_segments=K2)
    child_count = jax.ops.segment_sum(jnp.ones((K1,), jnp.float32), parent_ids, num_segments=K2)
    top_centroids = parent_total / child_count[:, None]
    dist_rows = math.gcd(row_total, 512)

    def measure(block_index):
        start = (block_index * dist_rows).astype(jnp.int32)
        features = lax.dynamic_slice_in_dim(embeddings, start, dist_rows, 0).astype(jnp.float32)
        picks = lax.dynamic_slice_in_dim(candidates, start, dist_rows, 1)
        gathered = rounded[picks].astype(jnp.float32)
        products = jnp.einsum("krd,rd->kr", gathered, features)
        feature_norms = jnp.sum(features * features, axis=1)
        return (feature_norms[None, :] - 2.0 * products + rounded_norms[picks]) / D

    blocks = lax.map(measure, jnp.arange(row_total // dist_rows, dtype=jnp.int32))
    candidate_dist = jnp.transpose(blocks, (1, 0, 2)).reshape(NCAND, row_total)
    return new_centroids, top_centroids, candidate_dist
```

```python
import functools

import jax
import jax.numpy as jnp
from jax import lax
from jax.experimental import pallas as pl
from jax.experimental.pallas import tpu as pltpu
from jax.sharding import PartitionSpec as P

MESH = pl.DeviceIdType.MESH
NT = (((1,), (1,)), ((), ()))
NX, NY, NZ = 4, 4, 8
D = 1024
W = D + 128
ROWS = 1024
K1 = 2048
K2 = 256
NCAND = 32


def encode(x):
    top = jnp.max(jnp.abs(x), axis=1, keepdims=True)
    t = jnp.ceil(jnp.log2(jnp.maximum(top, 1e-30) * (1.0 / 32700.0)) * 256.0)
    t = jnp.maximum(t, -30000.0)
    codes = jnp.round(x * jnp.exp2(t * (-1.0 / 256.0))).astype(jnp.int32).astype(jnp.int16)
    scale = jnp.broadcast_to(t, (x.shape[0], 128)).astype(jnp.int32).astype(jnp.int16)
    return codes, scale


def decode(block):
    wide = block.astype(jnp.int32).astype(jnp.float32)
    s = jnp.exp2(wide[:, D:] * (1.0 / 256.0))
    return jnp.concatenate([wide[:, j * 128 : (j + 1) * 128] * s for j in range(D // 128)], axis=1)


def exchange_kernel(
    emb, ids_ref, cent_ref, gathered,
    rows_buf, ids_far, part, own, cnt, cnt_in, s1, r1, s2, r2, zs, zr, mine,
    local_sem, send, recv, gsend, grecv,
):
    z = lax.axis_index("grp")
    o = lax.axis_index("own")
    c = lax.rem(o, 2)
    x = lax.rem(lax.div(o, 2), NX)
    y = lax.div(o, 2 * NX)

    def at(dx=0, dy=0, dz=0, flip=False):
        xx = lax.rem(x + dx + NX, NX)
        yy = lax.rem(y + dy + NY, NY)
        zz = lax.rem(z + dz + NZ, NZ)
        cc = 1 - c if flip else c
        return (zz, (yy * NX + xx) * 2 + cc)

    def along(axis, step):
        return at(dx=step) if axis == 0 else at(dy=step)

    peers = [at(flip=True)]
    peers += [at(dx=j) for j in (1, 2, 3)]
    peers += [at(dy=j) for j in (1, 2, 3)]
    peers += [at(dz=j) for j in range(1, NZ)]

    fetch = pltpu.make_async_copy(emb, rows_buf.at[pl.ds(0, ROWS)], local_sem.at[0])
    fetch.start()

    barrier = pltpu.get_barrier_semaphore()
    for peer in peers:
        pl.semaphore_signal(barrier, inc=1, device_id=peer, device_id_type=MESH)
    pl.semaphore_wait(barrier, len(peers))

    used = [0]

    def copy(src, dst, to):
        i = used[0]
        used[0] += 1
        return pltpu.make_async_remote_copy(
            src_ref=src, dst_ref=dst, send_sem=send.at[i], recv_sem=recv.at[i], device_id=to, device_id_type=MESH
        )

    sent = []

    def go(m):
        m.start()
        sent.append(m)
        return m

    far_ids = go(copy(ids_ref, ids_far, at(flip=True)))
    far = [
        go(copy(emb.at[pl.ds(q * 256, 256)], rows_buf.at[pl.ds(ROWS + q * 256, 256)], at(flip=True)))
        for q in range(4)
    ]

    place = (2, 1, 3, 0)

    def cluster_ids(g):
        r = lax.broadcasted_iota(jnp.int32, (256, 1), 0)
        k = lax.rem(lax.div(r, 32), 4)
        i = lax.rem(r, 32)
        xg = lax.rem(x + place[g], NX)
        yg = lax.rem(y + place[g], NY)
        first = ((k * NX + xg) * 2 + c) * 64 + i
        second = ((yg * NX + k) * 2 + c) * 64 + 32 + i
        return jnp.where(r < 128, first, second)

    def hot(g, ids):
        return jnp.where(ids[...] == cluster_ids(g), 1.0, 0.0).astype(jnp.bfloat16)

    ones = jnp.ones((8, ROWS), jnp.bfloat16)

    def tally(h):
        return lax.dot_general(ones, h, NT, preferred_element_type=jnp.float32)[0:1]

    fetch.wait()
    near = []
    for g in range(4):
        h = hot(g, ids_ref)
        near.append(tally(h))
        part[g] = jnp.dot(h, rows_buf[0:ROWS], preferred_element_type=jnp.float32)

    far_ids.wait_recv()
    for m in far:
        m.wait_recv()

    def pack(value_of, buf, rows):
        @pl.loop(0, rows // 16)
        def _(b):
            i = pl.multiple_of(b * 16, 16)
            codes, scale = encode(value_of(i))
            buf[pl.ds(i, 16), 0:D] = codes
            buf[pl.ds(i, 16), D:W] = scale

    msgs = {}
    for g in range(4):
        h = hot(g, ids_far)
        both = near[g] + tally(h)
        xg = lax.rem(x + place[g], NX)
        yg = lax.rem(y + place[g], NY)
        cnt[0, pl.ds(xg, 1)] = both[:, 0:128]
        cnt[0, pl.ds(4 + yg, 1)] = both[:, 128:256]
        part[g] += jnp.dot(h, rows_buf[ROWS : 2 * ROWS], preferred_element_type=jnp.float32)
        if g == 0:
            for colour in range(2):
                for d in range(2):
                    pack(lambda i: part[0, pl.ds(colour * 128 + d * 64 + i, 16)], s1.at[colour, d, 0], 64)
                    msgs[colour, d, 0] = go(copy(s1.at[colour, d, 0], r1.at[colour, d, 0], along(colour, 1 - 2 * d)))
        elif g < 3:
            d = g - 1
            for colour in range(2):
                pack(lambda i: part[g, pl.ds(colour * 128 + (1 - d) * 64 + i, 16)], s1.at[colour, d, 1], 64)
                msgs[colour, d, 1] = go(copy(s1.at[colour, d, 1], r1.at[colour, d, 1], along(colour, 1 - 2 * d)))

    cnt_x = [go(copy(cnt.at[0], cnt_in.at[j - 1], at(dx=j))) for j in (1, 2, 3)]

    for colour in range(2):
        for d in range(2):
            msgs[colour, d, 0].wait_recv()
            pack(
                lambda i: part[1 + d, pl.ds(colour * 128 + d * 64 + i, 16)] + decode(r1[colour, d, 0, pl.ds(i, 16)]),
                s1.at[colour, d, 2],
                64,
            )
            msgs[colour, d, 2] = go(copy(s1.at[colour, d, 2], r1.at[colour, d, 2], along(colour, 1 - 2 * d)))

    for m in cnt_x:
        m.wait_recv()
    cnt[1] = cnt[0] + cnt_in[0] + cnt_in[1] + cnt_in[2]
    cnt_y = [go(copy(cnt.at[1], cnt_in.at[2 + j], at(dy=j))) for j in (1, 2, 3)]

    for colour in range(2):
        for d in range(2):
            msgs[colour, d, 1].wait_recv()
    for colour in range(2):
        for d in range(2):
            msgs[colour, d, 2].wait_recv()

    @pl.loop(0, 8)
    def _(b):
        i = pl.multiple_of(b * 16, 16)
        for colour in range(2):
            v = part[3, pl.ds(colour * 128 + i, 16)]
            own[colour, pl.ds(i, 16)] = v

    for colour in range(2):
        for d in range(2):
            for kind, half in ((1, 1 - d), (2, d)):

                @pl.loop(0, 4)
                def _(b):
                    i = pl.multiple_of(b * 16, 16)
                    own[colour, pl.ds(half * 64 + i, 16)] += decode(r1[colour, d, kind, pl.ds(i, 16)])

    def seg(colour, step, half):
        along_other = y if colour == 0 else x
        k = lax.rem(along_other + step, 4)
        return pl.ds(pl.multiple_of(k * 32 + half * 16, 16), 16)

    m2 = {}
    for colour in range(2):
        axis = 1 - colour
        for d in range(2):
            pack(lambda i: own[colour, seg(colour, 2, d)], s2.at[colour, d, 0], 16)
            m2[colour, d, 0] = go(copy(s2.at[colour, d, 0], r2.at[colour, d, 0], along(axis, 1 - 2 * d)))
    for colour in range(2):
        axis = 1 - colour
        for d in range(2):
            pack(lambda i: own[colour, seg(colour, place[1 + d], 1 - d)], s2.at[colour, d, 1], 16)
            m2[colour, d, 1] = go(copy(s2.at[colour, d, 1], r2.at[colour, d, 1], along(axis, 1 - 2 * d)))
    for m in cnt_y:
        m.wait_recv()
    cnt[2] = cnt[1] + cnt_in[3] + cnt_in[4] + cnt_in[5]
    cnt_z = [go(copy(cnt.at[2], cnt_in.at[5 + j], at(dz=j))) for j in range(1, NZ)]
    for colour in range(2):
        axis = 1 - colour
        for d in range(2):
            m2[colour, d, 0].wait_recv()
            pack(
                lambda i: own[colour, seg(colour, place[1 + d], d)] + decode(r2[colour, d, 0]),
                s2.at[colour, d, 2],
                16,
            )
            m2[colour, d, 2] = go(copy(s2.at[colour, d, 2], r2.at[colour, d, 2], along(axis, 1 - 2 * d)))
    for colour in range(2):
        for d in range(2):
            m2[colour, d, 1].wait_recv()
            m2[colour, d, 2].wait_recv()
    for colour in range(2):
        for half in range(2):
            total = (
                own[colour, seg(colour, 0, half)]
                + decode(r2[colour, half, 2])
                + decode(r2[colour, 1 - half, 1])
            )
            base = colour * 32 + half * 16
            part[0, pl.ds(base, 16)] = total
            codes, scale = encode(total)
            for q in range(2):
                b = base // 8 + q
                zs[b, :, 0:D] = codes[q * 8 : q * 8 + 8]
                zs[b, :, D:W] = scale[q * 8 : q * 8 + 8]

    m3 = [go(copy(zs.at[lax.rem(z + j, NZ)], zr.at[j - 1], at(dz=j))) for j in range(1, NZ)]
    for m in cnt_z:
        m.wait_recv()
    count_sum = cnt[2]
    for j in range(1, NZ):
        count_sum += cnt_in[5 + j]
    cnt[3] = count_sum
    low = z < 4
    crow = jnp.where(low, x, 4 + y)
    cbase = jnp.where(low, y, x) * 32 + lax.rem(z, 4) * 8
    line = cnt[3, pl.ds(crow, 1)]
    lane = lax.broadcasted_iota(jnp.int32, (8, 128), 1)
    sub = lax.broadcasted_iota(jnp.int32, (8, 128), 0)
    counts = jnp.sum(jnp.where(lane == cbase + sub, jnp.broadcast_to(line, (8, 128)), 0.0), axis=1, keepdims=True)
    first = pl.multiple_of(z * 8, 8)
    total = part[0, pl.ds(first, 8)]
    for m, j in zip(m3, range(1, NZ)):
        m.wait_recv()
        total += decode(zr[j - 1])
    previous = cent_ref[pl.ds(first, 8)].astype(jnp.float32)
    new = jnp.where(counts > 0, total / jnp.maximum(counts, 1.0), previous)
    codes, scale = encode(new)
    mine[:, 0:D] = codes
    mine[:, D:W] = scale

    used_g = [0]

    def gcopy(ref, to, src=None):
        i = used_g[0]
        used_g[0] += 1
        return pltpu.make_async_remote_copy(
            src_ref=ref if src is None else src, dst_ref=ref,
            send_sem=gsend.at[i], recv_sem=grecv.at[i], device_id=to, device_id_type=MESH,
        )

    here = gathered.at[y, x, c, z]
    keep = pltpu.make_async_copy(mine, here, local_sem.at[1])
    keep.start()
    mz = [go(gcopy(here, at(dz=j), src=mine)) for j in range(1, NZ)]
    keep.wait()
    for m in mz:
        m.wait_recv()

    def block(colour, far1, far2, lo=0, n=4):
        a, b = lax.rem(y + (far1 if colour == 0 else far2), 4), lax.rem(x + (far2 if colour == 0 else far1), 4)
        return gathered.at[a, b, c, pl.ds(colour * 4 + lo, n)]

    to_core = []

    def share(ref):
        to_core.append(go(gcopy(ref, at(flip=True))))

    def first_axis(colour, d):
        return along(1 - colour, 1 - 2 * d)

    def second_axis(colour, d):
        return along(colour, 1 - 2 * d)

    step_a = {}
    step_b = {}
    for colour in range(2):
        for d in range(2):
            step_a[colour, d] = go(gcopy(block(colour, 0, 0), first_axis(colour, d)))
    for colour in range(2):
        for d in range(2):
            step_b[colour, 0, d] = go(gcopy(block(colour, 0, 0), second_axis(colour, d)))
    for colour in range(2):
        share(block(colour, 0, 0))
    origin = (3, 1)
    relay_a = {}
    for colour in range(2):
        for d in range(2):
            step_a[colour, d].wait_recv()
            relay_a[colour, d] = go(gcopy(block(colour, origin[d], 0, 2 * d, 2), first_axis(colour, d)))
    for colour in range(2):
        for d in range(2):
            for e in range(2):
                step_b[colour, origin[d], e] = go(gcopy(block(colour, origin[d], 0), second_axis(colour, e)))
            share(block(colour, origin[d], 0))
    relay_b = {}

    def arrived(colour, k):
        for e in range(2):
            step_b[colour, k, e].wait_recv()
            relay_b[colour, k, e] = go(gcopy(block(colour, k, origin[e], 2 * e, 2), second_axis(colour, e)))
            share(block(colour, k, origin[e]))

    for colour in range(2):
        arrived(colour, 0)
    for colour in range(2):
        for d in range(2):
            relay_a[colour, d].wait_recv()
        for e in range(2):
            step_b[colour, 2, e] = go(gcopy(block(colour, 2, 0), second_axis(colour, e)))
        share(block(colour, 2, 0))
    for k in (3, 1, 2):
        for colour in range(2):
            arrived(colour, k)
    for k in (0, 3, 1, 2):
        for colour in range(2):
            for e in range(2):
                relay_b[colour, k, e].wait_recv()
            share(block(colour, k, 2))
    for m in to_core:
        m.wait_recv()
    for m in sent:
        m.wait_send()


N_SEND = 60
N_GATHER = 100


def exchange(emb, ids, centroids):
    vmem = pl.BlockSpec(memory_space=pltpu.VMEM)
    hbm = pl.BlockSpec(memory_space=pl.ANY)
    i16 = jnp.int16
    return pl.pallas_call(
        exchange_kernel,
        out_shape=jax.ShapeDtypeStruct((NY, NX, 2, NZ, 8, W), i16),
        in_specs=[hbm, vmem, vmem],
        out_specs=hbm,
        scratch_shapes=[
            pltpu.VMEM((2 * ROWS, D), jnp.bfloat16),
            pltpu.VMEM((1, ROWS), jnp.int32),
            pltpu.VMEM((4, 256, D), jnp.float32),
            pltpu.VMEM((2, 128, D), jnp.float32),
            pltpu.VMEM((4, 8, 128), jnp.float32),
            pltpu.VMEM((13, 8, 128), jnp.float32),
            pltpu.VMEM((2, 2, 3, 64, W), i16),
            pltpu.VMEM((2, 2, 3, 64, W), i16),
            pltpu.VMEM((2, 2, 3, 16, W), i16),
            pltpu.VMEM((2, 2, 3, 16, W), i16),
            pltpu.VMEM((8, 8, W), i16),
            pltpu.VMEM((7, 8, W), i16),
            pltpu.VMEM((8, W), i16),
            pltpu.SemaphoreType.DMA((2,)),
            pltpu.SemaphoreType.DMA((N_SEND,)),
            pltpu.SemaphoreType.DMA((N_SEND,)),
            pltpu.SemaphoreType.DMA((N_GATHER,)),
            pltpu.SemaphoreType.DMA((N_GATHER,)),
        ],
        compiler_params=pltpu.CompilerParams(collective_id=0, has_side_effects=True, vmem_limit_bytes=48 << 20),
    )(emb, ids, centroids)


TILE = 256


def local_kernel(emb, cand, codes, parents, dist, top, new, rounded, norms):
    @pl.when(pl.program_id(0) == 0)
    def _():
        first = pl.multiple_of(lax.axis_index("own") * 64, 64)
        new[...] = decode(codes[pl.ds(first, 64)])
        top[...] = jnp.zeros_like(top)

        def chunk(b, children):
            i = pl.multiple_of(b * 256, 256)
            value = decode(codes[pl.ds(i, 256)])
            near = value.astype(jnp.bfloat16)
            wide = near.astype(jnp.float32)
            rest = (value - wide).astype(jnp.bfloat16)
            rounded[pl.ds(i, 256)] = near
            squares = jnp.zeros((256, 128), jnp.float32)
            for j in range(D // 128):
                v = wide[:, j * 128 : (j + 1) * 128]
                squares += v * v
            norms[:, pl.ds(i, 256)] = lax.dot_general(
                jnp.ones((8, 128), jnp.float32), squares, NT,
                precision=lax.Precision.HIGHEST, preferred_element_type=jnp.float32,
            )
            hot = jnp.where(
                parents[:, pl.ds(i, 256)] == lax.broadcasted_iota(jnp.int32, (K2, 256), 0), 1.0, 0.0
            )
            h = hot.astype(jnp.bfloat16)
            top[...] += jnp.dot(h, near, preferred_element_type=jnp.float32) + jnp.dot(
                h, rest, preferred_element_type=jnp.float32
            )
            return children + jnp.sum(hot, axis=1, keepdims=True)

        children = lax.fori_loop(0, K1 // 256, chunk, jnp.zeros((K2, 1), jnp.float32))
        top[...] = top[...] / children

    e = emb[...]
    wide = e.astype(jnp.float32)
    own_norm = jnp.sum(wide * wide, axis=1, keepdims=True)
    ids = jnp.concatenate([cand[...], jnp.zeros((128 - NCAND, TILE), jnp.int32)], axis=0)
    ids = jnp.concatenate([ids[:, q * 128 : (q + 1) * 128].T for q in range(TILE // 128)], axis=0)
    low = ids & 127
    high = ids >> 7
    acc = jnp.zeros((TILE, 128), jnp.float32)
    for b in range(K1 // 256):
        s = lax.dot_general(e, rounded[b * 256 : (b + 1) * 256], NT, preferred_element_type=jnp.float32)
        s = norms[0:1, b * 256 : (b + 1) * 256] - 2.0 * s
        for q in range(2):
            g = jnp.take_along_axis(s[:, q * 128 : (q + 1) * 128], low, axis=1, mode="promise_in_bounds")
            acc = jnp.where(high == 2 * b + q, g, acc)
    acc = (acc + own_norm) * (1.0 / D)
    dist[...] = jnp.concatenate([acc[q * 128 : (q + 1) * 128].T[0:NCAND] for q in range(TILE // 128)], axis=1)


def local(emb, cand, codes, parents):
    whole = lambda *shape: pl.BlockSpec(shape, lambda i: (0, 0), pipeline_mode=pl.Buffered(1))
    f32 = jnp.float32
    return pl.pallas_call(
        local_kernel,
        grid=(ROWS // TILE,),
        in_specs=[
            pl.BlockSpec((TILE, D), lambda i: (i, 0)),
            pl.BlockSpec((NCAND, TILE), lambda i: (0, i)),
            whole(K1, W),
            whole(1, K1),
        ],
        out_specs=[pl.BlockSpec((NCAND, TILE), lambda i: (0, i)), whole(K2, D), whole(64, D)],
        out_shape=[
            jax.ShapeDtypeStruct((NCAND, ROWS), f32),
            jax.ShapeDtypeStruct((K2, D), f32),
            jax.ShapeDtypeStruct((64, D), f32),
        ],
        scratch_shapes=[pltpu.VMEM((K1, D), jnp.bfloat16), pltpu.VMEM((8, K1), f32)],
        compiler_params=pltpu.CompilerParams(vmem_limit_bytes=48 << 20),
    )(emb, cand, codes, parents)


def per_device(embeddings, assign_one, candidates, centroids, parents):
    codes = exchange(embeddings, assign_one.reshape(1, ROWS), centroids)
    dist, top, new = local(embeddings, candidates, codes.reshape(K1, W), parents.reshape(1, K1))
    return new, top, dist


def solution(mesh):
    both = ("grp", "own")
    return jax.shard_map(
        per_device,
        mesh=mesh,
        in_specs=(P(both, None), P(both), P(None, both), P("own", None), P()),
        out_specs=(P("own", None), P(), P(None, both)),
        check_vma=False,
    )
```
